512 devices in a mesh: grp: 16 (over x, y), dev: 32 (over z, core).
Axes of the slice: x: 4, y: 4, z: 16, core: 2. Of those that a mesh axis runs over, the one named last changes fastest.
Arguments:
- coords: float32 [3, 65536], P(None, ('grp', 'dev')), may hold values from 0 to 1
- field: float32 [65536, 256], P(('grp', 'dev')), may hold values from -6 to 6
- observed: float32 [65536, 256], P(('grp', 'dev')), may hold values from -9 to 9
- pair_owner: int32 [16, 32], replicated, may hold values from 0 to 31, as said below
- cond_list: int32 [1024, 8], replicated, may hold values from 0 to 1023, as said below
- cond_mask: int32 [1024, 8], replicated, may hold values from 0 to 1, as said below
Outputs:
- field_out: float32 [65536, 256], P(('grp', 'dev'))
- last_grad: float32 [65536, 256], P(('grp', 'dev'))
The draws below stay inside these ranges and needn't reach their ends.
Inputs may be any that keep to these rules, and one draw needn't show every extreme that they name: `pair_owner`: each row is a permutation of the device indices. `cond_list`: a used slot s < 6 of block b names an earlier block of b's group, a used slot s >= 6 a block of the group before; padded slots hold 0; for every group g and devices p, q of it, the used slots of the blocks stored on device p of group g and of those stored on device p of group g + 1 that name blocks stored on device q of group g name one block at most, and no more than one slot names it; this bound is reached. `cond_mask`: blocks of the first group and early blocks of a group have padded slots.
All inputs are finite; a program needn't handle non-finite values.
Results may differ from the reference program's by a relative error of at most 0.0017.
Values may be sent and summed in bfloat16 or wider, within the bound.
A program may use at most 64 MiB of HBM per device.

```python
import jax
import jax.numpy as jnp
from jax import lax

PTS = 64
OUT = 256
NCOND = 8
NSAME = 6
STEPS = 2
NPTS = 65536
N_GRP = 16
N_DEV = 32


def owner_perm(key):
    keys = jax.random.split(jax.random.fold_in(key, 7), N_GRP)
    return jax.vmap(lambda single: jax.random.permutation(single, N_DEV))(keys).astype(jnp.int32)


def build_lists(key):
    group_members = N_DEV
    groups = N_GRP
    cross_covariance = NCOND - NSAME
    owning_device = owner_perm(key)
    row_ids = jnp.broadcast_to(jnp.arange(groups, dtype=jnp.int32)[:, None], (groups, group_members))
    inverse_factor = jnp.zeros((groups, group_members), jnp.int32).at[row_ids, owning_device].set(jnp.broadcast_to(jnp.arange(group_members, dtype=jnp.int32)[None, :], (groups, group_members)))
    cand_n = group_members + 2 * NCOND
    candidate_points = jnp.arange(cand_n, dtype=jnp.int32)
    pair_vals = jnp.arange(group_members, dtype=jnp.int32)[None, :, None]
    group_entries = jnp.arange(groups, dtype=jnp.int32)[:, None, None]
    score_one = jax.random.randint(jax.random.fold_in(key, 101), (groups, group_members, cand_n), 0, 2 ** 20) * cand_n + candidate_points
    score_one = score_one + (candidate_points[None, None, :] >= pair_vals).astype(jnp.int32) * 2 ** 28
    order_one = jnp.argsort(score_one, axis=-1)[..., :2 * NSAME].astype(jnp.int32)
    valid_one = jnp.broadcast_to(jnp.arange(2 * NSAME, dtype=jnp.int32)[None, None, :] < pair_vals, (groups, group_members, 2 * NSAME))
    half_one = jax.random.randint(jax.random.fold_in(key, 102), (groups, group_members, 2 * NSAME), 0, 2)
    same_ids = jnp.where(valid_one, group_entries * 2 * group_members + 2 * order_one + half_one, 0)
    same_ids = jnp.broadcast_to(same_ids, (groups, group_members, 2 * NSAME))
    preceding_group = jnp.maximum(jnp.arange(groups, dtype=jnp.int32) - 1, 0)
    forwarding_pair = inverse_factor[preceding_group[:, None], owning_device]
    score_two = jax.random.randint(jax.random.fold_in(key, 103), (groups, group_members, cand_n), 0, 2 ** 20) * cand_n + candidate_points
    blocked_points = (candidate_points[None, None, :] <= forwarding_pair[:, :, None]) | (candidate_points[None, None, :] >= group_members)
    score_two = score_two + blocked_points.astype(jnp.int32) * 2 ** 28
    order_two = jnp.argsort(score_two, axis=-1)[..., :2 * cross_covariance].astype(jnp.int32)
    second_valid = (jnp.arange(2 * cross_covariance, dtype=jnp.int32)[None, None, :] < group_members - 1 - forwarding_pair[:, :, None]) & (group_entries >= 1)
    second_valid = jnp.broadcast_to(second_valid, (groups, group_members, 2 * cross_covariance))
    half_two = jax.random.randint(jax.random.fold_in(key, 104), (groups, group_members, 2 * cross_covariance), 0, 2)
    cross_ids = jnp.where(second_valid, (group_entries - 1) * 2 * group_members + 2 * order_two + half_two, 0)
    cross_ids = jnp.broadcast_to(cross_ids, (groups, group_members, 2 * cross_covariance))
    ids = jnp.concatenate([same_ids.reshape(groups, group_members, 2, NSAME), cross_ids.reshape(groups, group_members, 2, cross_covariance)], axis=-1)
    mask = jnp.concatenate([valid_one.reshape(groups, group_members, 2, NSAME), second_valid.reshape(groups, group_members, 2, cross_covariance)], axis=-1)
    return (ids.reshape(groups * group_members * 2, NCOND).astype(jnp.int32), mask.reshape(groups * group_members * 2, NCOND).astype(jnp.int32))


def draw_pair_owner(key, part):
    return owner_perm(key)


def draw_cond_list(key, part):
    return build_lists(key)[0]


def draw_cond_mask(key, part):
    return build_lists(key)[1]


def steps_of(rng, extent, shards, low, largest):
    def one(dim, blocks):
        draws = jax.random.uniform(jax.random.fold_in(jax.random.fold_in(rng, 6), dim), (blocks,), jnp.float32, low / len(shards), largest / len(shards))
        return jnp.repeat(jnp.exp(draws), extent[dim] // blocks).reshape((-1,) + (1,) * (len(extent) - dim - 1))

    factor_of = one(*shards[0])
    for cut in shards[1:]:
        factor_of = factor_of * one(*cut)
    return factor_of


def scatter_about(stream_key, dims, width, most, cuts=(), kind=jnp.bfloat16):
    gain = steps_of(stream_key, dims, cuts, -0.22, 0.18) if cuts else 1.0
    array = jax.random.normal(stream_key, dims, jnp.float32) * width * gain
    return jnp.minimum(jnp.maximum(array, -most), most).astype(kind)


def setup_inputs(seed: int = 0) -> dict:
    arg_keys = jax.random.split(jax.random.key(seed), 7)
    return {
        "coords": jnp.clip(1.0 * jax.random.uniform(arg_keys[0], (3, NPTS), jnp.float32) ** steps_of(arg_keys[0], (3, NPTS), ((1, 512),), -0.2, 0.2), 0.0, 1.0),
        "field": scatter_about(arg_keys[1], (NPTS, OUT), 1.0, 6.0, ((0, 512),), jnp.float32),
        "observed": scatter_about(arg_keys[2], (NPTS, OUT), 1.5, 9.0, ((0, 512),), jnp.float32),
        "pair_owner": draw_pair_owner(jax.random.fold_in(arg_keys[6], 71), 0),
        "cond_list": draw_cond_list(jax.random.fold_in(arg_keys[6], 71), 0),
        "cond_mask": draw_cond_mask(jax.random.fold_in(arg_keys[6], 71), 0),
    }


HIGH = lax.Precision.HIGHEST
LENGTH_SCALE = 0.35
NUGGET = 0.5
STEP_SIZE = 0.3
BATCH_ROWS = 16

def kernel_of(first, second):
    dist_sq = jnp.zeros((first.shape[1], second.shape[1]), jnp.float32)
    for coord in range(3):
        diff = first[coord][:, None] - second[coord][None, :]
        dist_sq = dist_sq + diff * diff
    return jnp.exp(-jnp.sqrt(dist_sq) / LENGTH_SCALE)

def factor_block(own_x, cond_x, point_mask):
    kcc = kernel_of(cond_x, cond_x) * point_mask[:, None] * point_mask[None, :]
    kcc = kcc + jnp.diag(NUGGET * point_mask + (1.0 - point_mask))
    kci = kernel_of(cond_x, own_x) * point_mask[:, None]
    count = own_x.shape[1]
    kii = kernel_of(own_x, own_x) + NUGGET * jnp.eye(count, dtype=jnp.float32)
    lower = jnp.linalg.cholesky(kcc)
    whiten = lax.linalg.triangular_solve(lower, kci, left_side=True, lower=True)
    regress = lax.linalg.triangular_solve(lower, whiten, left_side=True, lower=True, transpose_a=True)
    cond_cov = kii - jnp.dot(whiten.T, whiten, precision=HIGH)
    low_cov = jnp.linalg.cholesky(cond_cov)
    inv_low = lax.linalg.triangular_solve(low_cov, jnp.eye(count, dtype=jnp.float32), left_side=True, lower=True)
    precision = jnp.dot(inv_low.T, inv_low, precision=HIGH)
    return (regress, precision)

def reference(coords, field, observed, pair_owner, cond_list, cond_mask):
    group_members = N_DEV
    nblocks = 2 * N_DEV * N_GRP
    block_ids = jnp.arange(nblocks, dtype=jnp.int32)
    group_of = block_ids // (2 * group_members)
    pair_of = block_ids % (2 * group_members) // 2
    half_of = block_ids % 2
    position = ((group_of * group_members + pair_owner[group_of, pair_of]) * 2 + half_of).astype(jnp.int32)
    all_x = coords.reshape(3, nblocks, PTS).transpose(1, 0, 2)[position]
    state = field.reshape(nblocks, PTS, OUT)[position]
    target = observed.reshape(nblocks, PTS, OUT)[position]
    mask_f = cond_mask.astype(jnp.float32)
    batches = nblocks // BATCH_ROWS

    def setup_one(own_x, ids, slot_mask):
        cond_x = all_x[ids].transpose(1, 0, 2).reshape(3, NCOND * PTS)
        return factor_block(own_x, cond_x, jnp.repeat(slot_mask, PTS))

    def setup_batch(args):
        return jax.vmap(setup_one)(*args)
    regress, precision = lax.map(setup_batch, (all_x.reshape(batches, BATCH_ROWS, 3, PTS), cond_list.reshape(batches, BATCH_ROWS, NCOND), mask_f.reshape(batches, BATCH_ROWS, NCOND)))
    regress = regress.reshape(nblocks, NCOND * PTS, PTS)
    precision = precision.reshape(nblocks, PTS, PTS)
    grad = jnp.zeros_like(state)
    for step_idx in range(STEPS):
        rounded = lax.optimization_barrier(state.astype(jnp.bfloat16)).astype(jnp.float32)

        def apply_one(own_f, ids, slot_mask, reg, prec):
            cond = (rounded[ids] * slot_mask[:, None, None]).reshape(NCOND * PTS, OUT)
            resid = own_f - jnp.dot(reg.T, cond, precision=HIGH)
            scaled = jnp.dot(prec, resid, precision=HIGH)
            back = jnp.dot(reg, scaled, precision=HIGH).reshape(NCOND, PTS, OUT) * slot_mask[:, None, None]
            return (scaled, back.astype(jnp.bfloat16))

        def apply_batch(args):
            return jax.vmap(apply_one)(*args)
        scaled, back = lax.map(apply_batch, (state.reshape(batches, BATCH_ROWS, PTS, OUT), cond_list.reshape(batches, BATCH_ROWS, NCOND), mask_f.reshape(batches, BATCH_ROWS, NCOND), regress.reshape(batches, BATCH_ROWS, NCOND * PTS, PTS), precision.reshape(batches, BATCH_ROWS, PTS, PTS)))
        scaled = scaled.reshape(nblocks, PTS, OUT)
        back = back.reshape(nblocks, NCOND, PTS, OUT)
        incoming = jnp.zeros((nblocks, PTS, OUT), jnp.float32)
        for slot in range(NCOND):
            incoming = incoming.at[cond_list[:, slot]].add(back[:, slot].astype(jnp.float32))
        grad = jnp.tanh(target - state) - (scaled - incoming)
        state = state + STEP_SIZE * grad
    field_out = jnp.zeros((nblocks, PTS, OUT), jnp.float32).at[position].set(state).reshape(nblocks * PTS, OUT)
    last_grad = jnp.zeros((nblocks, PTS, OUT), jnp.float32).at[position].set(grad).reshape(nblocks * PTS, OUT)
    return (field_out, last_grad)
```

```python
import jax
import jax.numpy as jnp
from jax import lax
from jax.experimental import pallas as pl
from jax.experimental.pallas import tpu as pltpu
from jax.sharding import PartitionSpec as P

NCOND = 8
NSAME = 6
STEPS = 2


HIGH = lax.Precision.HIGHEST
LENGTH_SCALE = 0.35
NUGGET = 0.5
STEP_SIZE = 0.3


def shifted(block, axis, distance):
    devices = range(lax.axis_size(axis))
    route = [(i - distance, i) for i in devices if i - distance in devices]
    return lax.ppermute(block, axis, route)


B = 64
F32 = jnp.float32
BF = jnp.bfloat16

def dot3(a, b, dims):
    return lax.dot_general(a, b, (dims, ((), ())), precision=HIGH, preferred_element_type=F32)


NN = ((1,), (0,))
NT = ((1,), (1,))

def diag_pair(block):
    both = jnp.concatenate([block, block], axis=0)
    row = lax.broadcasted_iota(jnp.int32, (2 * B, 2 * B), 0)
    lane = lax.broadcasted_iota(jnp.int32, (2 * B, 2 * B), 1)
    return jnp.where((row < B) == (lane < B), both, 0.0)

def invert_pair(a):
    tiles = [a[8 * t : 8 * t + 8] for t in range(8)]
    lane = lax.broadcasted_iota(jnp.int32, (8, 2 * B), 1)
    sub = lax.broadcasted_iota(jnp.int32, (8, 2 * B), 0)
    col = lane % B
    base = lane - col
    for k in range(0, B, 2):
        t, o = k // 8, k % 8
        c0 = [jnp.take_along_axis(x, base + k, axis=1) for x in tiles]
        c1 = [jnp.take_along_axis(x, base + k + 1, axis=1) for x in tiles]
        def bc(x, r):
            return jnp.broadcast_to(x[r : r + 1], (8, 2 * B))
        p, q, s = bc(c0[t], o), bc(c0[t], o + 1), bc(c1[t], o + 1)
        r0, r1 = bc(tiles[t], o), bc(tiles[t], o + 1)
        m0, m1 = col == k, col == k + 1
        r0 = jnp.where(m0, 1.0, jnp.where(m1, 0.0, r0))
        r1 = jnp.where(m1, 1.0, jnp.where(m0, 0.0, r1))
        inv = 1.0 / (p * s - q * q)
        s0 = (s * inv) * r0 - (q * inv) * r1
        s1 = (p * inv) * r1 - (q * inv) * r0
        keep = jnp.where(m0 | m1, 0.0, 1.0)
        new = [x * keep - c0[i] * s0 - c1[i] * s1 for i, x in enumerate(tiles)]
        new[t] = jnp.where(sub == o, s0, jnp.where(sub == o + 1, s1, new[t]))
        tiles = new
    return jnp.concatenate(tiles, axis=0)

def factor_kernel(xrow_ref, xcol_ref, reg_ref, prec_ref, s_ref):
    nb = xcol_ref.shape[0]
    lane = lax.broadcasted_iota(jnp.int32, (nb * B, 2 * B), 1)
    def wide(d):
        return jnp.where(lane < B, xrow_ref[:, d : d + 1], xrow_ref[:, 4 + d : 5 + d])
    rows = [wide(d) for d in range(4)]
    sub = lax.broadcasted_iota(jnp.int32, (B, 2 * B), 0)
    dcol = lax.broadcasted_iota(jnp.int32, (B, 2 * B), 1) % B
    for j in range(nb):
        sq = None
        for d in range(3):
            diff = rows[d][j * B :] - xcol_ref[j, d : d + 1]
            sq = diff * diff if sq is None else sq + diff * diff
        mask = xcol_ref[j, 3:4]
        k = jnp.exp(-jnp.sqrt(sq) / 0.35) * rows[3][j * B :] * mask
        s_ref[j, j * B :] = k
        s_ref[j, j * B : (j + 1) * B] = k[:B] + jnp.where(sub == dcol, 0.5 * mask + (1.0 - mask), 0.0)

    def step(j, carry):
        inv = invert_pair(s_ref[j, pl.ds(pl.multiple_of(j * B, B), B)])
        prec_ref[...] = inv
        big = diag_pair(inv)
        for jj in range(nb - 1):
            @pl.when(j == jj)
            def _():
                panel = s_ref[jj, (jj + 1) * B :]
                w = dot3(panel, big, NN)
                for i in range(jj + 1, nb):
                    o = (i - jj - 1) * B
                    s_ref[i, i * B :] -= dot3(w[o:], diag_pair(panel[o : o + B]), NT)
                s_ref[jj, (jj + 1) * B :] = w
        return carry
    lax.fori_loop(0, nb, step, 0)
    own = (nb - 1) * B
    rest = [s_ref[j, own:] for j in range(nb - 1)]
    for i in range(nb - 2, -1, -1):
        reg_ref[i] = rest[i]
        for j in range(i):
            rest[j] = rest[j] - dot3(rest[i], diag_pair(s_ref[j, i * B : (i + 1) * B]), NN)

def factor(xrow, xcol):
    nb = xcol.shape[0]
    return pl.pallas_call(
        factor_kernel,
        out_shape=(jax.ShapeDtypeStruct((nb - 1, B, 2 * B), F32), jax.ShapeDtypeStruct((B, 2 * B), F32)),
        in_specs=[pl.BlockSpec(memory_space=pltpu.VMEM)] * 2,
        out_specs=(pl.BlockSpec(memory_space=pltpu.VMEM),) * 2,
        scratch_shapes=[pltpu.VMEM((nb, nb * B, 2 * B), F32)],
    )(xrow, xcol)


def body(coords, field, observed, pair_owner, cond_list, cond_mask):
    groups = lax.axis_size("grp")
    group_members = lax.axis_size("dev")
    my_group = lax.axis_index("grp")
    my_member = lax.axis_index("dev")
    points = field.shape[0] // 2
    out_cols = field.shape[1]
    cross_covariance = NCOND - NSAME
    member_ids = jnp.arange(group_members, dtype=jnp.int32)
    halves = jnp.arange(2, dtype=jnp.int32)
    inverse_factor = jnp.sum(
        jnp.where(
            pair_owner[:, :, None] == member_ids[None, None, :], member_ids[None, :, None], 0
        ),
        axis=1,
    )
    all_lists = cond_list.reshape(groups, group_members, 2, NCOND)
    all_masks = cond_mask.reshape(groups, group_members, 2, NCOND)
    next_group = jnp.minimum(my_group + 1, groups - 1)
    has_next = (my_group + 1 < groups).astype(jnp.int32)
    owner_here = pair_owner[my_group]
    base_id = my_group * 2 * group_members

    def locate(targets):
        pair_idx = jnp.clip((targets - base_id) // 2, 0, group_members - 1)
        return (owner_here[pair_idx], targets % 2)

    here_lists = all_lists[my_group][inverse_factor[my_group]]
    here_masks = all_masks[my_group][inverse_factor[my_group]]
    next_lists = all_lists[next_group][inverse_factor[next_group]][:, :, NSAME:]
    next_masks = all_masks[next_group][inverse_factor[next_group]][:, :, NSAME:] * has_next
    same_owner, same_half = locate(here_lists[:, :, :NSAME])
    fwd_owner, fwd_half = locate(next_lists)
    same_hit = (here_masks[:, :, :NSAME] * (same_owner == my_member))[..., None] * (
        same_half[..., None] == halves
    )
    fwd_hit = (next_masks * (fwd_owner == my_member))[..., None] * (fwd_half[..., None] == halves)
    selector = (jnp.sum(same_hit, axis=(1, 2)) + jnp.sum(fwd_hit, axis=(1, 2))).astype(jnp.float32)
    select_bf = selector.astype(jnp.bfloat16)
    same_valid = here_masks[my_member][:, :NSAME].reshape(-1).astype(jnp.float32)
    fwd_valid = next_masks[my_member].reshape(-1).astype(jnp.float32)
    req_owner = jnp.concatenate(
        [same_owner[my_member].reshape(-1), fwd_owner[my_member].reshape(-1)]
    )
    req_half = jnp.concatenate([same_half[my_member].reshape(-1), fwd_half[my_member].reshape(-1)])
    req_valid = jnp.concatenate([same_valid, fwd_valid])
    req_row = 2 * req_owner + req_half
    my_mask = here_masks[my_member].astype(jnp.float32)
    onehot_same = (
        (same_owner[my_member].reshape(-1)[:, None] == member_ids[None, :]) * same_valid[:, None]
    ).astype(jnp.bfloat16)
    onehot_fwd = (
        (fwd_owner[my_member].reshape(-1)[:, None] == member_ids[None, :]) * fwd_valid[:, None]
    ).astype(jnp.bfloat16)
    own_x = coords.reshape(3, 2, points).transpose(1, 0, 2)
    send_x = (
        selector[:, 0, None, None] * own_x[0][None] + selector[:, 1, None, None] * own_x[1][None]
    )
    recv_x = lax.all_to_all(send_x, "dev", split_axis=0, concat_axis=0, tiled=True)
    got_x = recv_x[req_owner]
    same_x = got_x[: 2 * NSAME].reshape(2, NSAME, 3, points)
    lift_x = shifted(got_x[2 * NSAME :].reshape(2, cross_covariance, 3, points), "grp", 1)
    cond_x = jnp.concatenate([same_x, lift_x], axis=1)
    all_x = jnp.concatenate([cond_x, own_x[:, None]], axis=1)
    all_mask = jnp.concatenate([my_mask, jnp.ones((2, 1), jnp.float32)], axis=1)
    all_mask = jnp.broadcast_to(all_mask[:, :, None, None], (2, NCOND + 1, 1, points))
    full = jnp.concatenate([all_x, all_mask], axis=2)
    xrow = full.transpose(1, 3, 0, 2).reshape((NCOND + 1) * points, 8)
    xcol = full.transpose(1, 2, 0, 3).reshape(NCOND + 1, 4, 2 * points)
    reg, prec = factor(xrow, xcol)
    regress = reg.reshape(NCOND, points, 2, points).transpose(2, 0, 3, 1).reshape(2, NCOND * points, points)
    precision = prec.reshape(points, 2, points).transpose(1, 0, 2)
    state = field.reshape(2, points, out_cols)
    target = observed.reshape(2, points, out_cols)
    slot_mask = my_mask[:, :, None, None]
    grad = jnp.zeros_like(state)
    for step_idx in range(STEPS):
        rounded = state.astype(jnp.bfloat16)
        piece = lax.all_gather(rounded, "dev", axis=0, tiled=True)
        rows = jnp.arange(piece.shape[0], dtype=jnp.int32)
        hit = ((req_row[:, None] == rows[None, :]) * req_valid[:, None]).astype(jnp.bfloat16)
        got = jnp.einsum("rn,npo->rpo", hit, piece, preferred_element_type=jnp.float32).astype(
            jnp.bfloat16
        )
        same = got[: 2 * NSAME].reshape(2, NSAME, points, out_cols)
        lifted = shifted(got[2 * NSAME :].reshape(2, cross_covariance, points, out_cols), "grp", 1)
        cond = jnp.concatenate([same, lifted], axis=1).astype(jnp.float32) * slot_mask
        cond = cond.reshape(2, NCOND * points, out_cols)
        resid = state - jnp.einsum("hnp,hno->hpo", regress, cond, precision=HIGH)
        scaled = jnp.einsum("hpq,hqo->hpo", precision, resid, precision=HIGH)
        back = jnp.einsum("hnp,hpo->hno", regress, scaled, precision=HIGH).reshape(
            2, NCOND, points, out_cols
        )
        back = (back * slot_mask).astype(jnp.bfloat16)
        dropped = shifted(back[:, NSAME:], "grp", -1)
        outgo = jnp.einsum(
            "rq,rpo->qpo",
            onehot_same,
            back[:, :NSAME].reshape(2 * NSAME, points, out_cols),
            preferred_element_type=jnp.float32,
        )
        outgo = outgo + jnp.einsum(
            "rq,rpo->qpo",
            onehot_fwd,
            dropped.reshape(2 * cross_covariance, points, out_cols),
            preferred_element_type=jnp.float32,
        )
        returned = lax.all_to_all(
            outgo.astype(jnp.bfloat16), "dev", split_axis=0, concat_axis=0, tiled=True
        )
        incoming = jnp.einsum(
            "qh,qpo->hpo", select_bf, returned, preferred_element_type=jnp.float32
        )
        grad = jnp.tanh(target - state) - (scaled - incoming)
        state = state + STEP_SIZE * grad
    return (state.reshape(2 * points, out_cols), grad.reshape(2 * points, out_cols))


def solution(mesh):
    placed = (
        P(None, ("grp", "dev")),
        P(("grp", "dev"), None),
        P(("grp", "dev"), None),
        P(),
        P(),
        P(),
    )
    return jax.shard_map(
        body,
        mesh=mesh,
        in_specs=placed,
        out_specs=(P(("grp", "dev"), None), P(("grp", "dev"), None)),
        check_vma=False,
    )
```

```python
import jax
import jax.numpy as jnp
from jax import lax
from jax.experimental import pallas as pl
from jax.experimental.pallas import tpu as pltpu
from jax.sharding import PartitionSpec as P

NCOND = 8
NSAME = 6
NCROSS = NCOND - NSAME
STEPS = 2
HIGH = lax.Precision.HIGHEST
LENGTH_SCALE = 0.35
NUGGET = 0.5
STEP_SIZE = 0.3
MESH = pl.DeviceIdType.MESH
F32 = jnp.float32
BF16 = jnp.bfloat16
B = 64
NB = NCOND + 1
SLOTS = 2 * NCOND
FWD = 2 * NSAME
NFWD = 2 * NCROSS
NN = ((1,), (0,))
NT = ((1,), (1,))

MASK = SLOTS
HALF = MASK + SLOTS
SEL = 40


def offsets(chips):
    give = SEL + 4 * chips
    take = give + chips
    return give, take, take + 2 * chips


def dot(a, b, dims):
    return lax.dot_general(a, b, (dims, ((), ())), precision=HIGH, preferred_element_type=F32)


def table_kernel(owner_ref, list_ref, mask_ref, out_ref):
    members = owner_ref.shape[1]
    chips = members // 2
    give, take, size = offsets(chips)
    base = lax.axis_index("grp") * 2 * members
    me = lax.axis_index("dev")
    core = me % 2

    def clear(i, carry):
        out_ref[SEL + i] = SLOTS
        return carry

    lax.fori_loop(0, 5 * chips, clear, 0)

    def zero(i, carry):
        out_ref[take + i] = 0
        return carry

    lax.fori_loop(0, 2 * chips, zero, 0)
    for partner in (False, True):
        device = me + 1 - 2 * core if partner else me

        def find(group):
            def look(i, found):
                return found + jnp.where(owner_ref[group, i] == device, i, 0)

            return lax.fori_loop(0, members, look, 0)

        pair, next_pair = find(0), find(1)
        for half in range(2):
            for slot in range(NCOND):
                cross = slot >= NSAME
                group, row = (1, 2 * next_pair + half) if cross else (0, 2 * pair + half)
                block = list_ref[group, row, slot]
                used = mask_ref[group, row, slot]
                index = FWD + half * NCROSS + slot - NSAME if cross else half * NSAME + slot
                where = jnp.minimum(jnp.maximum((block - base) // 2, 0), members - 1)
                owner = owner_ref[0, where]
                side = block % 2
                if partner:

                    @pl.when((used == 1) & (owner % 2 == core))
                    def _():
                        out_ref[take + owner - core + side] = 1
                else:
                    out_ref[index] = 2 * owner + side
                    out_ref[MASK + half * NCOND + slot] = mask_ref[0, 2 * pair + half, slot]
                    if cross:
                        out_ref[HALF + half * NCROSS + slot - NSAME] = list_ref[0, 2 * pair + half, slot] % 2

                    @pl.when(used == 1)
                    def _():
                        out_ref[SEL + 2 * owner + side] = index

                    @pl.when((used == 1) & (owner % 2 != core))
                    def _():
                        out_ref[give + owner // 2] = index


def diag_pair(block):
    both = jnp.concatenate([block, block], axis=0)
    row = lax.broadcasted_iota(jnp.int32, (2 * B, 2 * B), 0)
    lane = lax.broadcasted_iota(jnp.int32, (2 * B, 2 * B), 1)
    return jnp.where((row < B) == (lane < B), both, 0.0)


def inverse2(p, q, s):
    inv = 1.0 / (p * s - q * q)
    a, b, c = s * inv, q * inv, p * inv
    return lambda x, y: (a * x - b * y, c * y - b * x)


def invert_pair(a):
    lane = lax.broadcasted_iota(jnp.int32, (B, 2 * B), 1)
    sub = lax.broadcasted_iota(jnp.int32, (B, 2 * B), 0)
    col = jnp.where(lane < B, lane, lane - B)
    for k in range(0, B, 4):
        c = [
            jnp.where(
                lane < B,
                jnp.broadcast_to(a[:, i : i + 1], (B, 2 * B)),
                jnp.broadcast_to(a[:, B + i : B + i + 1], (B, 2 * B)),
            )
            for i in range(k, k + 4)
        ]
        pivot = (col >= k) & (col < k + 4)

        def g(i, j):
            return c[j][k + i : k + i + 1]

        r = [
            jnp.where(col[:1] == k + i, 1.0, jnp.where(pivot[:1], 0.0, a[k + i : k + i + 1]))
            for i in range(4)
        ]
        first = inverse2(g(0, 0), g(1, 0), g(1, 1))
        v0, v1 = first(r[0], r[1])
        g02, g12 = first(g(0, 2), g(1, 2))
        g03, g13 = first(g(0, 3), g(1, 3))
        second = inverse2(
            g(2, 2) - (g(0, 2) * g02 + g(1, 2) * g12),
            g(3, 2) - (g(0, 3) * g02 + g(1, 3) * g12),
            g(3, 3) - (g(0, 3) * g03 + g(1, 3) * g13),
        )
        s2, s3 = second(r[2] - (g(0, 2) * v0 + g(1, 2) * v1), r[3] - (g(0, 3) * v0 + g(1, 3) * v1))
        s0 = v0 - (g02 * s2 + g03 * s3)
        s1 = v1 - (g12 * s2 + g13 * s3)
        a = jnp.where(pivot, 0.0, a) - (c[0] * s0 + c[1] * s1) - (c[2] * s2 + c[3] * s3)
        for i, solved in enumerate((s0, s1, s2, s3)):
            a = jnp.where(sub == k + i, solved, a)
    return a


def main_kernel(
    tab, x_ref, f_ref, y_ref, field_ref, grad_ref,
    cx, fxs, fx, xcol, xrow, s_ref, prec_ref, reg_ref, regt_ref, state, scaled,
    everyone, fwd, got, back, home, give_buf, take_buf, out_buf, in_buf,
    cs, cr, cps, cpr, xfs, xfr, gs, gr, ps, pr, fs, fr, bs, br, vs, vr, rs, rr,
):
    members = cx.shape[0]
    chips = members // 2
    hops = chips // 2
    give, take, size = offsets(chips)
    groups = lax.axis_size("grp")
    group = lax.axis_index("grp")
    me = lax.axis_index("dev")
    core = me % 2
    chip = me // 2

    def around(step):
        return (chip + step + chips) % chips

    right = (group, 2 * around(1) + core)
    left = (group, 2 * around(-1) + core)
    toward = (right, left)
    sign = (1, -1)
    partner = (group, me + 1 - 2 * core)
    after = ((group + 1) % groups, me)
    before = ((group + groups - 1) % groups, me)

    barrier = pltpu.get_barrier_semaphore()
    for peer in (right, left, partner, after, before):
        pl.semaphore_signal(barrier, inc=1, device_id=peer, device_id_type=MESH)
    pl.semaphore_wait(barrier, 5)

    def copy(src, dst, send, recv, peer):
        return pltpu.make_async_remote_copy(
            src_ref=src, dst_ref=dst, send_sem=send, recv_sem=recv, device_id=peer, device_id_type=MESH
        )

    def coord_hop(d, hop):
        src = x_ref if hop == 1 else cx.at[2 * around(-sign[d] * (hop - 1)) + core]
        dst = cx.at[2 * around(-sign[d] * (hop - 1)) + core]
        return copy(src, dst, cs.at[d, hop - 1], cr.at[d, hop - 1], toward[d])

    def coord_got(d, hop):
        ref = cx.at[2 * around(-sign[d] * hop) + core]
        return copy(ref, ref, cs.at[d, hop - 1], cr.at[d, hop - 1], toward[d])

    def coord_pass(d, hop):
        ref = cx.at[2 * around(-sign[d] * hop) + core]
        return copy(ref, ref, cps.at[d, hop], cpr.at[d, hop], partner)

    def coord_passed(d, hop):
        ref = cx.at[2 * around(-sign[d] * hop) + 1 - core]
        return copy(ref, ref, cps.at[d, hop], cpr.at[d, hop], partner)

    def ways(hop):
        return (0, 1) if hop < hops else (0,)

    for d in ways(1):
        coord_hop(d, 1).start()
    copy(x_ref, cx.at[me], cps.at[0, 0], cpr.at[0, 0], partner).start()
    cx[me] = x_ref[...]

    def gather_send(st, d, hop, half):
        ref = everyone.at[st, 4 * around(-sign[d] * (hop - 1)) + 2 * core + half]
        return copy(ref, ref, gs.at[d, hop - 1, half], gr.at[d, hop - 1, half], toward[d])

    def gather_got(st, d, hop, half):
        ref = everyone.at[st, 4 * around(-sign[d] * hop) + 2 * core + half]
        return copy(ref, ref, gs.at[d, hop - 1, half], gr.at[d, hop - 1, half], toward[d])

    def gather_pass(st, d, hop, half):
        ref = everyone.at[st, 4 * around(-sign[d] * hop) + 2 * core + half]
        return copy(ref, ref, ps.at[d, hop, half], pr.at[d, hop, half], partner)

    def gather_passed(st, d, hop, half):
        ref = everyone.at[st, 4 * around(-sign[d] * hop) + 2 * (1 - core) + half]
        return copy(ref, ref, ps.at[d, hop, half], pr.at[d, hop, half], partner)

    def lanes(hop):
        return [(d, half) for half in range(2) for d in range(2) if hop < hops or d == half]

    def gather_begin(st):
        for half in range(2):
            everyone[st, 2 * me + half] = state[half].astype(BF16)
        for d, half in lanes(1):
            gather_send(st, d, 1, half).start()
        for half in range(2):
            gather_pass(st, 0, 0, half).start()

    def gather_next(st, hop):
        for d, half in lanes(hop):
            gather_got(st, d, hop, half).wait_recv()
            if hop < hops and (d, half) in lanes(hop + 1):
                gather_send(st, d, hop + 1, half).start()
            gather_pass(st, d, hop, half).start()

    def gather_end(st):
        for half in range(2):
            gather_passed(st, 0, 0, half).wait()
        for hop in range(1, hops + 1):
            for d, half in lanes(hop):
                gather_passed(st, d, hop, half).wait()
                gather_send(st, d, hop, half).wait_send()

    def forward(st):
        for i in range(NFWD):
            fwd[st, i] = everyone[st, tab[FWD + i]]
            copy(fwd.at[st, i], got.at[st, i], fs.at[i], fr.at[i], after).start()

    def forwarded(st):
        for i in range(NFWD):
            copy(fwd.at[st, i], got.at[st, i], fs.at[i], fr.at[i], after).wait()

    state[...] = f_ref[...]
    for hop in range(1, hops + 1):
        for d in ways(hop):
            coord_got(d, hop).wait_recv()
            if hop < hops and d in ways(hop + 1):
                coord_hop(d, hop + 1).start()
            coord_pass(d, hop).start()
    coord_passed(0, 0).wait()
    for hop in range(1, hops + 1):
        for d in ways(hop):
            coord_passed(d, hop).wait()
            coord_hop(d, hop).wait_send()
    for i in range(NFWD):
        fxs[i] = cx[tab[FWD + i] // 2]
        copy(fxs.at[i], fx.at[i], xfs.at[i], xfr.at[i], after).start()
    gather_begin(0)
    for i in range(NFWD):
        copy(fxs.at[i], fx.at[i], xfs.at[i], xfr.at[i], after).wait()

    lane8 = lax.broadcasted_iota(jnp.int32, (8, 2 * B), 1)
    sub8 = lax.broadcasted_iota(jnp.int32, (8, 2 * B), 0)
    lane = lax.broadcasted_iota(jnp.int32, (B, 2 * B), 1)
    sub = lax.broadcasted_iota(jnp.int32, (B, 2 * B), 0)
    point = jnp.where(lane < B, lane, lane - B)

    def mask(half, slot):
        return tab[MASK + half * NCOND + slot].astype(F32)

    for j in range(NB):
        if j == NCOND:
            placed = jnp.where(sub8 == 3, 1.0, x_ref[...])
        else:
            sides = []
            for half in range(2):
                if j < NSAME:
                    row = tab[half * NSAME + j]
                    found, side = cx[row // 2], row % 2
                else:
                    i = half * NCROSS + j - NSAME
                    found, side = fx[i], tab[HALF + i]
                turned = jnp.concatenate([found[:, B:], found[:, :B]], axis=1)
                same = (side == half).astype(F32)
                sides.append(found * same + turned * (1.0 - same))
            placed = jnp.where(lane8 < B, sides[0], sides[1])
            weights = jnp.where(lane8 < B, mask(0, j), mask(1, j))
            placed = jnp.where(sub8 == 3, weights, placed)
        xcol[j] = placed
        standing = placed.T
        for d in range(4):
            xrow[d, j * B : (j + 1) * B] = jnp.where(
                lane < B, standing[:B, d : d + 1], standing[B:, d : d + 1]
            )
    for j in range(NB):
        sq = None
        for d in range(3):
            diff = xrow[d, j * B :] - xcol[j, d : d + 1]
            sq = diff * diff if sq is None else sq + diff * diff
        weights = xcol[j, 3:4]
        s_ref[j, j * B :] = jnp.exp(-jnp.sqrt(sq) / LENGTH_SCALE) * xrow[3, j * B :] * weights
        s_ref[j, j * B : (j + 1) * B] += jnp.where(
            sub == point, NUGGET * weights + (1.0 - weights), 0.0
        )

    def eliminate(j, carry):
        inv = invert_pair(s_ref[j, pl.ds(pl.multiple_of(j * B, B), B)])
        prec_ref[...] = inv
        big = diag_pair(inv)
        for jj in range(NCOND):

            @pl.when(j == jj)
            def _():
                if 1 <= jj <= hops:
                    gather_next(0, jj)
                panel = s_ref[jj, (jj + 1) * B :]
                w = dot(panel, big, NN)
                for i in range(jj + 1, NB):
                    o = (i - jj - 1) * B
                    s_ref[i, i * B :] -= dot(w[o:], diag_pair(panel[o : o + B]), NT)
                s_ref[jj, (jj + 1) * B :] = w

        return carry

    lax.fori_loop(0, NB, eliminate, 0)
    for hop in range(NCOND, hops + 1):
        gather_next(0, hop)
    gather_end(0)
    forward(0)
    own = NCOND * B
    rest = [s_ref[j, own:] for j in range(NCOND)]
    for i in range(NCOND - 1, -1, -1):
        turned = rest[i].T
        for half in range(2):
            reg_ref[half, :, i * B : (i + 1) * B] = rest[i][:, half * B : (half + 1) * B]
            regt_ref[half, i * B : (i + 1) * B] = turned[half * B : (half + 1) * B]
        for j in range(i):
            rest[j] = rest[j] - dot(rest[i], diag_pair(s_ref[j, i * B : (i + 1) * B]), NN)

    for st in range(STEPS):
        if st:
            gather_begin(st)
            for hop in range(1, hops + 1):
                gather_next(st, hop)
            gather_end(st)
            forward(st)
        forwarded(st)
        for half in range(2):
            cond = [
                everyone[st, tab[half * NSAME + s]].astype(F32) * mask(half, s) for s in range(NSAME)
            ] + [
                got[st, half * NCROSS + s].astype(F32) * mask(half, NSAME + s) for s in range(NCROSS)
            ]
            resid = state[half] - dot(reg_ref[half], jnp.concatenate(cond, axis=0), NN)
            solved = dot(prec_ref[:, half * B : (half + 1) * B], resid, NN)
            scaled[half] = solved
            terms = dot(regt_ref[half], solved, NN)
            for s in range(NCOND):
                term = (terms[s * B : (s + 1) * B] * mask(half, s)).astype(BF16)
                if s < NSAME:
                    back[st, half * NSAME + s] = term
                else:
                    home[st, half * NCROSS + s - NSAME] = term
        for i in range(NFWD):
            copy(home.at[st, i], back.at[st, FWD + i], bs.at[i], br.at[i], before).start()
        back[st, SLOTS] = jnp.zeros((B, back.shape[3]), BF16)
        for i in range(NFWD):
            copy(home.at[st, i], back.at[st, FWD + i], bs.at[i], br.at[i], before).wait()

        order = [around(hops)]
        for step in range(hops - 1, 0, -1):
            order += [around(step), around(-step)]
        order.append(chip)

        def given(n):
            ref = give_buf.at[st, n]
            return copy(ref, take_buf.at[st, n], vs.at[n], vr.at[n], partner)

        for n, dest in enumerate(order):
            give_buf[st, n] = back[st, tab[give + dest]]
            given(n).start()

        def owed(n, half):
            dest = order[n]
            mine = back[st, tab[SEL + 4 * dest + 2 * core + half]].astype(F32)
            return mine + take_buf[st, n].astype(F32) * tab[take + 2 * dest + half].astype(F32)

        def carried(d, hop, half):
            return copy(
                out_buf.at[st, d, hop - 1, half], in_buf.at[st, d, hop - 1, half],
                rs.at[d, hop - 1, half], rr.at[d, hop - 1, half], toward[d],
            )

        def starts(hop):
            return [(d, half) for half in range(2) for d in range(2) if hop > 1 or d == half]

        given(0).wait_recv()
        for hop in range(1, hops + 1):
            if hop > 1:
                for d in range(2):
                    given(2 * hop - 3 + d).wait_recv()
            for d, half in starts(hop):
                total = owed(0 if hop == 1 else 2 * hop - 3 + d, half)
                if hop > 1 and (d, half) in starts(hop - 1):
                    carried(d, hop - 1, half).wait_recv()
                    total = total + in_buf[st, d, hop - 2, half].astype(F32)
                out_buf[st, d, hop - 1, half] = total.astype(BF16)
                carried(d, hop, half).start()
        last = 2 * hops - 1
        given(last).wait_recv()
        for half in range(2):
            incoming = owed(last, half)
            for d in range(2):
                if (d, half) in starts(hops):
                    carried(d, hops, half).wait_recv()
                    incoming = incoming + in_buf[st, d, hops - 1, half].astype(F32)
            now = state[half]
            grad = jnp.tanh(y_ref[half] - now) - (scaled[half] - incoming)
            state[half] = now + STEP_SIZE * grad
            grad_ref[half] = grad
        for n in range(2 * hops):
            given(n).wait_send()
        for hop in range(1, hops + 1):
            for d, half in starts(hop):
                carried(d, hop, half).wait_send()
    field_ref[...] = state[...]


def body(coords, field, observed, pair_owner, cond_list, cond_mask):
    groups = lax.axis_size("grp")
    members = lax.axis_size("dev")
    chips = members // 2
    hops = chips // 2
    group = lax.axis_index("grp")
    following = jnp.minimum(group + 1, groups - 1)
    has_next = (group + 1 < groups).astype(jnp.int32)
    cols = field.shape[1]
    lists = cond_list.reshape(groups, 2 * members, NCOND)
    masks = cond_mask.reshape(groups, 2 * members, NCOND)

    def both(array):
        return jnp.stack([array[group], array[following]])

    masks = both(masks) * jnp.stack([jnp.int32(1), has_next])[:, None, None]
    size = offsets(chips)[2]
    smem = pl.BlockSpec(memory_space=pltpu.SMEM)
    vmem = pl.BlockSpec(memory_space=pltpu.VMEM)
    table = pl.pallas_call(
        table_kernel,
        out_shape=jax.ShapeDtypeStruct((size,), jnp.int32),
        in_specs=[smem] * 3,
        out_specs=smem,
        name="tables",
    )(both(pair_owner), both(lists), masks)
    x = jnp.pad(coords, ((0, 5), (0, 0)))
    sem = pltpu.SemaphoreType.DMA
    block = (B, cols)
    shape = (2, B, cols)
    out = pl.pallas_call(
        main_kernel,
        out_shape=(jax.ShapeDtypeStruct(shape, F32), jax.ShapeDtypeStruct(shape, F32)),
        in_specs=[smem, vmem, vmem, vmem],
        out_specs=(vmem, vmem),
        scratch_shapes=[
            pltpu.VMEM((members, 8, 2 * B), F32),
            pltpu.VMEM((NFWD, 8, 2 * B), F32),
            pltpu.VMEM((NFWD, 8, 2 * B), F32),
            pltpu.VMEM((NB, 8, 2 * B), F32),
            pltpu.VMEM((4, NB * B, 2 * B), F32),
            pltpu.VMEM((NB, NB * B, 2 * B), F32),
            pltpu.VMEM((B, 2 * B), F32),
            pltpu.VMEM((2, B, NCOND * B), F32),
            pltpu.VMEM((2, NCOND * B, B), F32),
            pltpu.VMEM(shape, F32),
            pltpu.VMEM(shape, F32),
            pltpu.VMEM((STEPS, 2 * members) + block, BF16),
            pltpu.VMEM((STEPS, NFWD) + block, BF16),
            pltpu.VMEM((STEPS, NFWD) + block, BF16),
            pltpu.VMEM((STEPS, SLOTS + 1) + block, BF16),
            pltpu.VMEM((STEPS, NFWD) + block, BF16),
            pltpu.VMEM((STEPS, chips) + block, BF16),
            pltpu.VMEM((STEPS, chips) + block, BF16),
            pltpu.VMEM((STEPS, 2, hops, 2) + block, BF16),
            pltpu.VMEM((STEPS, 2, hops, 2) + block, BF16),
            sem((2, hops)), sem((2, hops)),
            sem((2, hops + 1)), sem((2, hops + 1)),
            sem((NFWD,)), sem((NFWD,)),
            sem((2, hops, 2)), sem((2, hops, 2)),
            sem((2, hops + 1, 2)), sem((2, hops + 1, 2)),
            sem((NFWD,)), sem((NFWD,)),
            sem((NFWD,)), sem((NFWD,)),
            sem((chips,)), sem((chips,)),
            sem((2, hops, 2)), sem((2, hops, 2)),
        ],
        compiler_params=pltpu.CompilerParams(
            collective_id=0, has_side_effects=True, vmem_limit_bytes=48 * 1024 * 1024
        ),
        name="vecchia",
    )(table, x, field.reshape(shape), observed.reshape(shape))
    return tuple(array.reshape(2 * B, cols) for array in out)


def solution(mesh):
    placed = (
        P(None, ("grp", "dev")),
        P(("grp", "dev"), None),
        P(("grp", "dev"), None),
        P(),
        P(),
        P(),
    )
    return jax.shard_map(
        body,
        mesh=mesh,
        in_specs=placed,
        out_specs=(P(("grp", "dev"), None), P(("grp", "dev"), None)),
        check_vma=False,
    )
```

```python
import jax
import jax.numpy as jnp
from jax import lax
from jax.experimental import pallas as pl
from jax.experimental.pallas import tpu as pltpu
from jax.sharding import PartitionSpec as P

NCOND = 8
NSAME = 6
NCROSS = NCOND - NSAME
STEPS = 2
HIGH = lax.Precision.HIGHEST
LENGTH_SCALE = 0.35
NUGGET = 0.5
STEP_SIZE = 0.3
MESH = pl.DeviceIdType.MESH
F32 = jnp.float32
BF16 = jnp.bfloat16
B = 64
NB = NCOND + 1
SLOTS = 2 * NCOND
FWD = 2 * NSAME
NFWD = 2 * NCROSS
NN = ((1,), (0,))
NT = ((1,), (1,))

MASK = SLOTS
HALF = MASK + SLOTS
SEL = 40


def offsets(chips):
    give = SEL + 4 * chips
    take = give + chips
    return give, take, take + 2 * chips


def dot(a, b, dims):
    return lax.dot_general(a, b, (dims, ((), ())), precision=HIGH, preferred_element_type=F32)


def plain(a, b):
    return jnp.dot(a, b, preferred_element_type=F32)


def split(a):
    high = a.astype(BF16)
    return high, (a - high.astype(F32)).astype(BF16)


def diag_pair(block):
    both = jnp.concatenate([block, block], axis=0)
    row = lax.broadcasted_iota(jnp.int32, (2 * B, 2 * B), 0)
    lane = lax.broadcasted_iota(jnp.int32, (2 * B, 2 * B), 1)
    return jnp.where((row < B) == (lane < B), both, 0.0)


def inverse2(p, q, s):
    inv = 1.0 / (p * s - q * q)
    a, b, c = s * inv, q * inv, p * inv
    return lambda x, y: (a * x - b * y, c * y - b * x)


def invert_pair(a):
    lane = lax.broadcasted_iota(jnp.int32, (B, 2 * B), 1)
    col = jnp.where(lane < B, lane, lane - B)
    col8 = col[:8]
    sub8 = lax.broadcasted_iota(jnp.int32, (8, 2 * B), 0)

    def row(x, i):
        return jnp.broadcast_to(x[i : i + 1], (8, 2 * B))

    def tall(x):
        return jnp.concatenate([x] * (B // 8), axis=0)

    for k in range(0, B, 4):
        c = [
            jnp.where(
                lane < B,
                jnp.broadcast_to(a[:, i : i + 1], (B, 2 * B)),
                jnp.broadcast_to(a[:, B + i : B + i + 1], (B, 2 * B)),
            )
            for i in range(k, k + 4)
        ]
        entry = {(i, j): row(c[j], k + i) for i in range(4) for j in range(i + 1)}

        def g(i, j):
            return entry[max(i, j), min(i, j)]

        pivot = (col >= k) & (col < k + 4)
        r = [
            jnp.where(col8 == k + i, 1.0, jnp.where(pivot[:8], 0.0, row(a, k + i))) for i in range(4)
        ]
        first = inverse2(g(0, 0), g(1, 0), g(1, 1))
        g02, g12 = first(g(0, 2), g(1, 2))
        g03, g13 = first(g(0, 3), g(1, 3))
        second = inverse2(
            g(2, 2) - (g(0, 2) * g02 + g(1, 2) * g12),
            g(3, 2) - (g(0, 3) * g02 + g(1, 3) * g12),
            g(3, 3) - (g(0, 3) * g03 + g(1, 3) * g13),
        )
        v0, v1 = first(r[0], r[1])
        s2, s3 = second(r[2] - (g(0, 2) * v0 + g(1, 2) * v1), r[3] - (g(0, 3) * v0 + g(1, 3) * v1))
        s0 = v0 - (g02 * s2 + g03 * s3)
        s1 = v1 - (g12 * s2 + g13 * s3)
        a = (
            jnp.where(pivot, 0.0, a)
            - (c[0] * tall(s0) + c[1] * tall(s1))
            - (c[2] * tall(s2) + c[3] * tall(s3))
        )
        top = k // 8 * 8
        rows = a[top : top + 8]
        for i, solved in enumerate((s0, s1, s2, s3)):
            rows = jnp.where(sub8 == k - top + i, solved, rows)
        a = jnp.concatenate([p for p in (a[:top], rows, a[top + 8 :]) if p.shape[0]], axis=0)
    return a


def main_kernel(
    owner_ref, list_ref, mask_ref, x_ref, f_ref, y_ref, field_ref, grad_ref, tab, keys,
    cx, fxs, fx, xcol, xrow, s_ref, prec_ref, reg_ref, regt_ref, state, scaled,
    everyone, fwd, got, back, home, give_buf, take_buf, out_buf, in_buf,
    cs, cr, cps, cpr, xfs, xfr, gs, gr, ps, pr, fs, fr, bs, br, vs, vr, rs, rr,
):
    members = cx.shape[0]
    chips = members // 2
    hops = chips // 2
    give, take, size = offsets(chips)
    groups = lax.axis_size("grp")
    group = lax.axis_index("grp")
    me = lax.axis_index("dev")
    core = me % 2
    chip = me // 2

    def around(step):
        return (chip + step + chips) % chips

    def along(step, side):
        return (group, 2 * around(step) + side)

    sign = (1, -1)
    partner = along(0, 1 - core)
    after = ((group + 1) % groups, me)
    before = ((group + groups - 1) % groups, me)
    reach = min(4, hops)

    barrier = pltpu.get_barrier_semaphore()
    near = [along(way * step, side) for step in range(1, reach + 1) for way in sign for side in range(2)]
    for peer in near + [partner, after, before]:
        pl.semaphore_signal(barrier, inc=1, device_id=peer, device_id_type=MESH)
    pl.semaphore_wait(barrier, len(near) + 3)

    def copy(src, dst, send, recv, peer):
        return pltpu.make_async_remote_copy(
            src_ref=src, dst_ref=dst, send_sem=send, recv_sem=recv, device_id=peer, device_id_type=MESH
        )

    def coord_send(d, dist, side):
        start = reach * ((dist - 1) // reach)
        place = 2 * around(-sign[d] * start) + core
        src = cx.at[place] if start else x_ref
        return copy(
            src, cx.at[place], cs.at[d, dist - 1, side], cr.at[d, dist - 1, core],
            along(sign[d] * (dist - start), side),
        )

    def coord_got(d, dist, side):
        ref = cx.at[2 * around(-sign[d] * dist) + side]
        return copy(ref, ref, cs.at[d, dist - 1, side], cr.at[d, dist - 1, side], partner)

    paths = [(d, dist) for dist in range(hops, 0, -1) for d in range(2) if dist < hops or d == 0]
    for d, dist in paths:
        if dist <= reach:
            for side in range(2):
                coord_send(d, dist, side).start()
    copy(x_ref, cx.at[me], cps.at[0], cpr.at[0], partner).start()
    cx[me] = x_ref[...]

    base = group * 2 * members

    def find(which, device):
        def look(i, found):
            return jnp.where(owner_ref[which, i] == device, i, found)

        return lax.fori_loop(0, members, look, 0)

    for other in range(2):
        device = me + 1 - 2 * core if other else me
        pair, next_pair = find(0, device), find(1, device)
        for half in range(2):
            for slot in range(NCOND):
                which, row = (0, 2 * pair + half) if slot < NSAME else (1, 2 * next_pair + half)
                block = list_ref[which, slot, row]
                used = mask_ref[which, slot, row]
                spot = jnp.minimum(jnp.maximum((block - base) // 2, 0), members - 1)
                stored = 2 * owner_ref[0, spot] + block % 2
                index = half * NSAME + slot if slot < NSAME else FWD + half * NCROSS + slot - NSAME
                keys[other * SLOTS + index] = jnp.where(used == 1, stored, -1)
                if not other:
                    tab[index] = stored
                    tab[MASK + half * NCOND + slot] = mask_ref[0, slot, 2 * pair + half]
                    if slot >= NSAME:
                        tab[HALF + half * NCROSS + slot - NSAME] = list_ref[0, slot, 2 * pair + half] % 2

    def owe(i, carry):
        found = SLOTS
        for r in range(SLOTS):
            found = jnp.where(keys[r] == i, r, found)
        tab[SEL + i] = found
        return carry

    lax.fori_loop(0, 2 * members, owe, 0)

    def trade(i, carry):
        far = SEL + 4 * i + 2 * (1 - core)
        tab[give + i] = jnp.minimum(tab[far], tab[far + 1])
        for half in range(2):
            hit = 0
            for r in range(SLOTS):
                hit = jnp.where(keys[SLOTS + r] == 4 * i + 2 * core + half, 1, hit)
            tab[take + 2 * i + half] = hit
        return carry

    lax.fori_loop(0, chips, trade, 0)

    def gather_send(st, d, hop, half):
        start = 2 * ((hop - 1) // 2)
        ref = everyone.at[st, 4 * around(-sign[d] * start) + 2 * core + half]
        return copy(
            ref, ref, gs.at[d, hop - 1, half], gr.at[d, hop - 1, half],
            along(sign[d] * (hop - start), core),
        )

    def gather_got(st, d, hop, half):
        ref = everyone.at[st, 4 * around(-sign[d] * hop) + 2 * core + half]
        return copy(ref, ref, gs.at[d, hop - 1, half], gr.at[d, hop - 1, half], partner)

    def gather_pass(st, d, hop, half):
        ref = everyone.at[st, 4 * around(-sign[d] * hop) + 2 * core + half]
        return copy(ref, ref, ps.at[d, hop, half], pr.at[d, hop, half], partner)

    def gather_passed(st, d, hop, half):
        ref = everyone.at[st, 4 * around(-sign[d] * hop) + 2 * (1 - core) + half]
        return copy(ref, ref, ps.at[d, hop, half], pr.at[d, hop, half], partner)

    def lanes(hop):
        return [(d, half) for half in range(2) for d in range(2) if hop < hops or d == half]

    def gather_begin(st):
        for half in range(2):
            everyone[st, 2 * me + half] = state[half].astype(BF16)
        for hop in (2, 1):
            for d, half in lanes(hop):
                gather_send(st, d, hop, half).start()
        for half in range(2):
            gather_pass(st, 0, 0, half).start()

    def gather_next(st, hop):
        for d, half in lanes(hop):
            gather_got(st, d, hop, half).wait_recv()
            if hop < hops:
                if (d, half) in lanes(hop + 2):
                    gather_send(st, d, hop + 2, half).start()
                gather_send(st, d, hop + 1, half).start()
            gather_pass(st, d, hop, half).start()
        for d, half in lanes(hop - 1):
            gather_got(st, d, hop - 1, half).wait_recv()
            gather_pass(st, d, hop - 1, half).start()

    def gather_end(st):
        for half in range(2):
            gather_passed(st, 0, 0, half).wait()
        for hop in range(1, hops + 1):
            for d, half in lanes(hop):
                gather_passed(st, d, hop, half).wait()
                gather_send(st, d, hop, half).wait_send()

    def forward(st):
        for i in range(NFWD):
            fwd[st, i] = everyone[st, tab[FWD + i]]
            copy(fwd.at[st, i], got.at[st, i], fs.at[i], fr.at[i], after).start()

    def forwarded(st):
        for i in range(NFWD):
            copy(fwd.at[st, i], got.at[st, i], fs.at[i], fr.at[i], after).wait()

    state[...] = f_ref[...]
    for d, dist in paths:
        if dist <= reach:
            for side in range(2):
                coord_got(d, dist, side).wait_recv()
            if dist == reach and hops > reach:
                for far in range(hops, reach, -1):
                    if (d, far) in paths:
                        for side in range(2):
                            coord_send(d, far, side).start()
    for d, dist in paths:
        if dist > reach:
            for side in range(2):
                coord_got(d, dist, side).wait_recv()
    other = cx.at[me + 1 - 2 * core]
    copy(other, other, cps.at[0], cpr.at[0], partner).wait()
    for d, dist in paths:
        for side in range(2):
            coord_send(d, dist, side).wait_send()
    for i in range(NFWD):
        fxs[i] = cx[tab[FWD + i] // 2]
        copy(fxs.at[i], fx.at[i], xfs.at[i], xfr.at[i], after).start()
    gather_begin(0)

    lane8 = lax.broadcasted_iota(jnp.int32, (8, 2 * B), 1)
    sub8 = lax.broadcasted_iota(jnp.int32, (8, 2 * B), 0)
    lane = lax.broadcasted_iota(jnp.int32, (B, 2 * B), 1)
    sub = lax.broadcasted_iota(jnp.int32, (B, 2 * B), 0)
    point = jnp.where(lane < B, lane, lane - B)

    def mask(half, slot):
        return tab[MASK + half * NCOND + slot].astype(F32)

    def stand(j):
        if j == NCOND:
            placed = jnp.where(sub8 == 3, 1.0, x_ref[...])
        else:
            sides = []
            for half in range(2):
                if j < NSAME:
                    row = tab[half * NSAME + j]
                    found, side = cx[row // 2], row % 2
                else:
                    i = half * NCROSS + j - NSAME
                    found, side = fx[i], tab[HALF + i]
                turned = jnp.concatenate([found[:, B:], found[:, :B]], axis=1)
                same = (side == half).astype(F32)
                sides.append(found * same + turned * (1.0 - same))
            placed = jnp.where(lane8 < B, sides[0], sides[1])
            weights = jnp.where(lane8 < B, mask(0, j), mask(1, j))
            placed = jnp.where(sub8 == 3, weights, placed)
        xcol[j] = placed
        standing = placed.T
        for d in range(4):
            xrow[d, j * B : (j + 1) * B] = jnp.where(
                lane < B, standing[:B, d : d + 1], standing[B:, d : d + 1]
            )
    def fill(j, low, high):
        sq = None
        for d in range(3):
            diff = xrow[d, low * B : high * B] - xcol[j, d : d + 1]
            sq = diff * diff if sq is None else sq + diff * diff
        weights = xcol[j, 3:4]
        s_ref[j, low * B : high * B] = (
            jnp.exp(-jnp.sqrt(sq) / LENGTH_SCALE) * xrow[3, low * B : high * B] * weights
        )
        if low == j:
            s_ref[j, j * B : (j + 1) * B] += jnp.where(
                sub == point, NUGGET * weights + (1.0 - weights), 0.0
            )

    early = list(range(NSAME)) + [NCOND]
    for j in early:
        stand(j)
    for j in early:
        if j < NSAME:
            fill(j, j, NSAME)
        fill(j, NCOND, NB)
    for i in range(NFWD):
        copy(fxs.at[i], fx.at[i], xfs.at[i], xfr.at[i], after).wait()
    for j in range(NSAME, NCOND):
        stand(j)
    for j in range(NCOND):
        if j < NSAME:
            fill(j, NSAME, NCOND)
        else:
            fill(j, j, NB)

    def eliminate(j, carry):
        inv = invert_pair(s_ref[j, pl.ds(pl.multiple_of(j * B, B), B)])
        prec_ref[...] = inv
        big = diag_pair(inv)
        for jj in range(NCOND):

            @pl.when(j == jj)
            def _():
                if 1 <= jj <= hops // 2:
                    gather_next(0, 2 * jj)
                panel = s_ref[jj, (jj + 1) * B :]
                w = dot(panel, big, NN)
                for i in range(jj + 1, NB):
                    o = (i - jj - 1) * B
                    s_ref[i, i * B :] -= dot(w[o:], diag_pair(panel[o : o + B]), NT)
                s_ref[jj, (jj + 1) * B :] = w

        return carry

    lax.fori_loop(0, NB, eliminate, 0)
    gather_end(0)
    forward(0)
    own = NCOND * B
    rest = [s_ref[j, own:] for j in range(NCOND)]
    for i in range(NCOND - 1, -1, -1):
        kept = rest[i] * jnp.where(lane < B, mask(0, i), mask(1, i))
        turned = kept.T
        for half in range(2):
            high, low = split(kept[:, half * B : (half + 1) * B])
            reg_ref[half, :B, i * B : (i + 1) * B] = high
            reg_ref[half, B:, i * B : (i + 1) * B] = low
            high, low = split(turned[half * B : (half + 1) * B])
            for part, values in enumerate((high, low, high)):
                regt_ref[half, i * B : (i + 1) * B, part * B : (part + 1) * B] = values
        for j in range(i):
            rest[j] = rest[j] - dot(rest[i], diag_pair(s_ref[j, i * B : (i + 1) * B]), NN)

    for st in range(STEPS):
        if st:
            gather_begin(st)
            for hop in range(2, hops + 1, 2):
                gather_next(st, hop)
            gather_end(st)
            forward(st)
        width = NSAME * B

        def seen(cond, first, last):
            both = plain(reg_ref[half, :, first:last], jnp.concatenate(cond, axis=0))
            return both[:B] + both[B:]

        def stacked(values):
            high, low = split(values)
            return jnp.concatenate([high, high, low], axis=0)

        for half in range(2):
            cond = [everyone[st, tab[half * NSAME + s]] for s in range(NSAME)]
            scaled[half] = state[half] - seen(cond, 0, width)
        forwarded(st)
        parts = []
        for half in range(2):
            cond = [got[st, half * NCROSS + s] for s in range(NCROSS)]
            resid = scaled[half] - seen(cond, width, NCOND * B)
            solved = dot(prec_ref[:, half * B : (half + 1) * B], resid, NN)
            scaled[half] = solved
            parts.append(stacked(solved))
            terms = plain(regt_ref[half, width:], parts[half])
            for s in range(NCROSS):
                i = half * NCROSS + s
                home[st, i] = terms[s * B : (s + 1) * B].astype(BF16)
                copy(home.at[st, i], back.at[st, FWD + i], bs.at[i], br.at[i], before).start()
        for half in range(2):
            terms = plain(regt_ref[half, :width], parts[half])
            for s in range(NSAME):
                back[st, half * NSAME + s] = terms[s * B : (s + 1) * B].astype(BF16)
        back[st, SLOTS] = jnp.zeros((B, back.shape[3]), BF16)
        for i in range(NFWD):
            copy(home.at[st, i], back.at[st, FWD + i], bs.at[i], br.at[i], before).wait()

        order = [around(hops)]
        for step in range(hops - 1, 0, -1):
            order += [around(step), around(-step)]
        order.append(chip)

        def given(n):
            ref = give_buf.at[st, n]
            return copy(ref, take_buf.at[st, n], vs.at[n], vr.at[n], partner)

        for n, dest in enumerate(order):
            give_buf[st, n] = back[st, tab[give + dest]]
            given(n).start()

        def owed(n, half):
            dest = order[n]
            mine = back[st, tab[SEL + 4 * dest + 2 * core + half]].astype(F32)
            return mine + take_buf[st, n].astype(F32) * tab[take + 2 * dest + half].astype(F32)

        def carried(d, hop, half):
            return copy(
                out_buf.at[st, d, hop - 1, half], in_buf.at[st, d, hop - 1, half],
                rs.at[d, hop - 1, half], rr.at[d, hop - 1, half],
                along(sign[d] * (2 - hop % 2), core),
            )

        def starts(hop):
            return [(d, half) for half in range(2) for d in range(2) if hop < hops or d == half]

        def arrived(d, hop, half):
            carried(d, hop, half).wait_recv()
            return in_buf[st, d, hop - 1, half].astype(F32)

        def place(d, hop):
            return 0 if hop == hops else 2 * (hops - hop) - 1 + d

        for hop in range(hops, 0, -1):
            for n in sorted({place(d, hop) for d in range(2)}):
                given(n).wait_recv()
            for d, half in starts(hop):
                total = owed(place(d, hop), half)
                if hop % 2 == 0 and hop < hops:
                    total = total + arrived(d, hop + 1, half)
                    if (d, half) in starts(hop + 2):
                        total = total + arrived(d, hop + 2, half)
                out_buf[st, d, hop - 1, half] = total.astype(BF16)
                carried(d, hop, half).start()
        last = 2 * hops - 1
        given(last).wait_recv()
        for half in range(2):
            incoming = owed(last, half)
            for d in range(2):
                for hop in (1, 2):
                    if (d, half) in starts(hop):
                        incoming = incoming + arrived(d, hop, half)
            now = state[half]
            grad = jnp.tanh(y_ref[half] - now) - (scaled[half] - incoming)
            state[half] = now + STEP_SIZE * grad
            grad_ref[half] = grad
        for n in range(2 * hops):
            given(n).wait_send()
        for hop in range(1, hops + 1):
            for d, half in starts(hop):
                carried(d, hop, half).wait_send()
    field_ref[...] = state[...]


def body(coords, field, observed, pair_owner, cond_list, cond_mask):
    groups = lax.axis_size("grp")
    members = lax.axis_size("dev")
    chips = members // 2
    hops = chips // 2
    group = lax.axis_index("grp")
    following = jnp.minimum(group + 1, groups - 1)
    has_next = (group + 1 < groups).astype(jnp.int32)
    cols = field.shape[1]
    lists = cond_list.reshape(groups, 2 * members, NCOND).transpose(0, 2, 1)
    masks = cond_mask.reshape(groups, 2 * members, NCOND).transpose(0, 2, 1)

    def both(array):
        return jnp.stack([array[group], array[following]])

    masks = both(masks) * jnp.stack([jnp.int32(1), has_next])[:, None, None]
    size = offsets(chips)[2]
    smem = pl.BlockSpec(memory_space=pltpu.SMEM)
    vmem = pl.BlockSpec(memory_space=pltpu.VMEM)
    x = jnp.pad(coords, ((0, 5), (0, 0)))
    sem = pltpu.SemaphoreType.DMA
    block = (B, cols)
    shape = (2, B, cols)
    out = pl.pallas_call(
        main_kernel,
        out_shape=(jax.ShapeDtypeStruct(shape, F32), jax.ShapeDtypeStruct(shape, F32)),
        in_specs=[smem, smem, smem, vmem, vmem, vmem],
        out_specs=(vmem, vmem),
        scratch_shapes=[
            pltpu.SMEM((size,), jnp.int32),
            pltpu.SMEM((2 * SLOTS,), jnp.int32),
            pltpu.VMEM((members, 8, 2 * B), F32),
            pltpu.VMEM((NFWD, 8, 2 * B), F32),
            pltpu.VMEM((NFWD, 8, 2 * B), F32),
            pltpu.VMEM((NB, 8, 2 * B), F32),
            pltpu.VMEM((4, NB * B, 2 * B), F32),
            pltpu.VMEM((NB, NB * B, 2 * B), F32),
            pltpu.VMEM((B, 2 * B), F32),
            pltpu.VMEM((2, 2 * B, NCOND * B), BF16),
            pltpu.VMEM((2, NCOND * B, 3 * B), BF16),
            pltpu.VMEM(shape, F32),
            pltpu.VMEM(shape, F32),
            pltpu.VMEM((STEPS, 2 * members) + block, BF16),
            pltpu.VMEM((STEPS, NFWD) + block, BF16),
            pltpu.VMEM((STEPS, NFWD) + block, BF16),
            pltpu.VMEM((STEPS, SLOTS + 1) + block, BF16),
            pltpu.VMEM((STEPS, NFWD) + block, BF16),
            pltpu.VMEM((STEPS, chips) + block, BF16),
            pltpu.VMEM((STEPS, chips) + block, BF16),
            pltpu.VMEM((STEPS, 2, hops, 2) + block, BF16),
            pltpu.VMEM((STEPS, 2, hops, 2) + block, BF16),
            sem((2, hops, 2)), sem((2, hops, 2)),
            sem((1,)), sem((1,)),
            sem((NFWD,)), sem((NFWD,)),
            sem((2, hops, 2)), sem((2, hops, 2)),
            sem((2, hops + 1, 2)), sem((2, hops + 1, 2)),
            sem((NFWD,)), sem((NFWD,)),
            sem((NFWD,)), sem((NFWD,)),
            sem((chips,)), sem((chips,)),
            sem((2, hops, 2)), sem((2, hops, 2)),
        ],
        compiler_params=pltpu.CompilerParams(
            collective_id=0, has_side_effects=True, vmem_limit_bytes=48 * 1024 * 1024
        ),
        name="vecchia",
    )(both(pair_owner), both(lists), masks, x, field.reshape(shape), observed.reshape(shape))
    return tuple(array.reshape(2 * B, cols) for array in out)


def solution(mesh):
    placed = (
        P(None, ("grp", "dev")),
        P(("grp", "dev"), None),
        P(("grp", "dev"), None),
        P(),
        P(),
        P(),
    )
    return jax.shard_map(
        body,
        mesh=mesh,
        in_specs=placed,
        out_specs=(P(("grp", "dev"), None), P(("grp", "dev"), None)),
        check_vma=False,
    )
```
